128 devices in a mesh: section: 2 (over x_lo), dp: 16 (over x_hi, y, core), mp: 4 (over z).
Axes of the slice: x: 4 (x_hi: 2, x_lo: 2; x = x_hi * 2 + x_lo), y: 4, z: 4, core: 2. Of those that a mesh axis runs over, the one named last changes fastest.
Arguments:
- hidden: bfloat16 [2, 16, 256, 5120], P('section', 'dp'), may hold values from -6 to 6
- gain: float32 [2, 5120], P('section'), may hold values from 0.5 to 2
- w_first: bfloat16 [2, 5120, 2560], P('section', 'dp', 'mp'), may hold values from -0.078125 to 0.078125
- w_second: bfloat16 [2, 5120, 2560], P('section', 'dp', 'mp'), may hold values from -0.078125 to 0.078125
- lengths: int32 [16, 2], P('dp'), may hold values from 32 to 256, as said below
- cotangent: bfloat16 [2, 16, 256, 5120], P('section', 'dp'), may hold values from -6 to 6
Outputs:
- result: bfloat16 [2, 16, 256, 5120], P('section', 'dp')
- d_hidden: bfloat16 [2, 16, 256, 5120], P('section', 'dp')
- d_gain: float32 [2, 5120], P('section', 'dp')
- d_first: float32 [2, 5120, 2560], P('section', 'dp', 'mp')
- d_second: float32 [2, 5120, 2560], P('section', 'dp', 'mp')
The draws below stay inside these ranges and needn't reach their ends.
Inputs may be any that keep to these rules, and one draw needn't show every extreme that they name: `lengths`: each row's source count and target count; positions at or past a count are padding.
All inputs are finite; a program needn't handle non-finite values.
Results may differ from the reference program's by a relative error of at most 0.017.
Values may be sent and summed in bfloat16 or wider, within the bound.
A program may use at most 128 MiB of HBM per device.

```python
import math
import jax
import jax.numpy as jnp
from jax import lax

D = 5120
HEAD = 128
SEQS = 1
LEN = 256
HD = 2560
BATCH = 16
N_DP = 16


def draw_gain(key, part):
    return jax.random.uniform(key, (2, D), jnp.float32, 0.5, 1.5)


def draw_lengths(key, part):
    lowest = max(LEN // 8, 1)
    counts = jax.random.randint(key, (BATCH, 2), lowest, LEN + 1)
    shuffled = jax.random.permutation(jax.random.fold_in(key, 11), BATCH)
    counts = counts.at[shuffled[0]].set(LEN)
    counts = counts.at[shuffled[1]].set(lowest)
    return counts.astype(jnp.int32)


def spiked(drawn, rng, source, target, parts, factor):
    owner, partner = [(jnp.arange(drawn.shape[dim]) // (drawn.shape[dim] // parts)).reshape([-1 if axis == dim else 1 for axis in range(drawn.ndim)]) for dim in (source, target)]
    chosen = jax.random.permutation(rng, parts)[partner]
    strong = (owner == chosen) | (owner == (partner + parts // 2) % parts)
    return jnp.where(strong, factor * drawn, drawn)


def shard_levels(stream_key, dims, shards, least, largest):
    level, own = 1.0, jax.random.fold_in(stream_key, 6)
    for position, parts in shards:
        draws = jnp.exp(jax.random.uniform(jax.random.fold_in(own, position), (parts,), jnp.float32, least / len(shards), largest / len(shards)))
        level = level * jnp.repeat(draws, dims[position] // parts).reshape([-1 if axis == position else 1 for axis in range(len(dims))])
    return level


def centred(rng, dims, deviation, reach, split=(), kind=jnp.bfloat16):
    level = shard_levels(rng, dims, split, -0.22, 0.18) if split else 1.0
    drawn = jax.random.normal(rng, dims, jnp.float32) * deviation * level
    return jnp.minimum(jnp.maximum(drawn, -reach), reach).astype(kind)


def noise_with(key, shape, scale, most, cuts, heavy, kind=jnp.bfloat16):
    array = scale * jax.random.normal(key, shape, jnp.float32)
    if cuts:
        array = array * shard_levels(key, shape, cuts, -0.22, 0.18)
    return jnp.clip(spiked(array, jax.random.fold_in(key, 3), *heavy), -most, most).astype(kind)


def setup_inputs(seed: int = 0) -> dict:
    seeds = jax.random.split(jax.random.key(seed), 7)
    hidden = noise_with(seeds[0], (2, BATCH, LEN, D), 1.0, 6.0, ((0, 2), (1, 16)), (1, 3, 16, 2.0))
    gain = draw_gain(jax.random.fold_in(seeds[6], 71), 0)
    w_first = centred(seeds[2], (2, D, HD), D ** -0.5, 0.078125, ((0, 2), (1, 16), (2, 4)))
    w_second = centred(seeds[3], (2, D, HD), D ** -0.5, 0.078125, ((0, 2), (1, 16), (2, 4)))
    lengths = draw_lengths(jax.random.fold_in(seeds[6], 71), 0)
    cotangent = centred(seeds[5], (2, BATCH, LEN, D), 1.0, 6.0, ((0, 2), (1, 16)))
    return dict(hidden=hidden, gain=gain, w_first=w_first, w_second=w_second, lengths=lengths, cotangent=cotangent)


EPS = 1e-06
MASKED = -1e+30

def normalize(states):
    wide = states.astype(jnp.float32)
    inverse = lax.rsqrt(lax.optimization_barrier(jnp.mean(wide * wide, axis=-1, keepdims=True)) + EPS)
    return (wide * inverse, inverse)

def project(left, right):
    flat = left.reshape(-1, left.shape[-1])
    return jnp.dot(flat, right, preferred_element_type=jnp.float32).reshape(left.shape[:-1] + (right.shape[-1],))

def project_back(left, right):
    flat = left.reshape(-1, left.shape[-1])
    return jnp.dot(flat, right.T, preferred_element_type=jnp.float32).reshape(left.shape[:-1] + (right.shape[0],))

def grouped_outer(left, right):
    span = SEQS * LEN
    left_rows = left.reshape(-1, left.shape[-1])
    right_rows = right.reshape(-1, right.shape[-1])
    total = jnp.zeros((left_rows.shape[1], right_rows.shape[1]), jnp.float32)
    for member in range(N_DP):
        piece = jnp.dot(left_rows[member * span:(member + 1) * span].T, right_rows[member * span:(member + 1) * span], preferred_element_type=jnp.float32)
        total = total + lax.optimization_barrier(piece.astype(jnp.bfloat16)).astype(jnp.float32)
    return total

def grouped_vector(product):
    pieces = lax.optimization_barrier(jnp.sum(product.reshape(N_DP, SEQS * LEN, product.shape[-1]), axis=1))
    pieces = lax.optimization_barrier(pieces.astype(jnp.bfloat16)).astype(jnp.float32)
    return lax.optimization_barrier(jnp.sum(pieces, axis=0))

def split_heads(values_in):
    batch_size, length, columns = values_in.shape
    return values_in.astype(jnp.float32).reshape(batch_size, length, columns // HEAD, HEAD)

def attend(queries, keys, values, key_count):
    batch_size, length, columns = queries.shape
    scale = 1.0 / math.sqrt(HEAD)
    scores = jnp.einsum('bqhd,bkhd->bhqk', split_heads(queries), split_heads(keys)) * scale
    visible = jnp.arange(length)[None, None, None, :] < key_count[:, None, None, None]
    scores = jnp.where(visible, scores, MASKED)
    weights = jax.nn.softmax(scores, axis=-1)
    weights_low = weights.astype(jnp.bfloat16)
    context = jnp.einsum('bhqk,bkhd->bqhd', weights_low.astype(jnp.float32), split_heads(values))
    return (context.reshape(batch_size, length, columns).astype(jnp.bfloat16), weights, weights_low)

def attend_back(grad_context, queries, keys, values, weights, weights_low):
    batch_size, length, columns = queries.shape
    scale = 1.0 / math.sqrt(HEAD)
    grad_heads = split_heads(grad_context)
    grad_weights = jnp.einsum('bqhd,bkhd->bhqk', grad_heads, split_heads(values))
    grad_values = jnp.einsum('bhqk,bqhd->bkhd', weights_low.astype(jnp.float32), grad_heads)
    centered = grad_weights - lax.optimization_barrier(jnp.sum(weights * grad_weights, axis=-1, keepdims=True))
    grad_scores = (weights * centered * scale).astype(jnp.bfloat16).astype(jnp.float32)
    grad_queries = jnp.einsum('bhqk,bkhd->bqhd', grad_scores, split_heads(keys))
    grad_keys = jnp.einsum('bhqk,bqhd->bkhd', grad_scores, split_heads(queries))
    shape_out = (batch_size, length, columns)
    return (grad_queries.reshape(shape_out).astype(jnp.bfloat16), grad_keys.reshape(shape_out).astype(jnp.bfloat16), grad_values.reshape(shape_out).astype(jnp.bfloat16))

def norm_back(grad_normed, unit, inverse, gains):
    scaled = grad_normed * gains
    inner = lax.optimization_barrier(jnp.mean(scaled * unit, axis=-1, keepdims=True))
    return inverse * (scaled - unit * inner)

def reference(hidden, gain, w_first, w_second, lengths, cotangent):
    enc_unit, enc_inverse = normalize(hidden[0])
    dec_unit, dec_inverse = normalize(hidden[1])
    memory = (enc_unit * gain[0]).astype(jnp.bfloat16)
    dec_normed = (dec_unit * gain[1]).astype(jnp.bfloat16)
    keys = project(memory, w_first[0]).astype(jnp.bfloat16)
    values = project(memory, w_second[0]).astype(jnp.bfloat16)
    queries = project(dec_normed, w_first[1]).astype(jnp.bfloat16)
    context, weights, weights_low = attend(queries, keys, values, lengths[:, 0])
    output = (hidden[1].astype(jnp.float32) + project_back(context, w_second[1])).astype(jnp.bfloat16)
    keep = jnp.arange(LEN)[None, :] < lengths[:, 1][:, None]
    grad_out = jnp.where(keep[:, :, None], cotangent[1], jnp.zeros((), cotangent.dtype))
    grad_context = project(grad_out, w_second[1]).astype(jnp.bfloat16)
    grad_queries, grad_keys, grad_values = attend_back(grad_context, queries, keys, values, weights, weights_low)
    d_first = jnp.stack([grouped_outer(memory, grad_keys), grouped_outer(dec_normed, grad_queries)])
    d_second = jnp.stack([grouped_outer(memory, grad_values), grouped_outer(grad_out, context)])
    enc_grad = cotangent[0].astype(jnp.float32) + project_back(grad_keys, w_first[0]) + project_back(grad_values, w_second[0])
    dec_grad = project_back(grad_queries, w_first[1])
    d_gain = jnp.stack([grouped_vector(enc_grad * enc_unit), grouped_vector(dec_grad * dec_unit)])
    enc_states = norm_back(enc_grad, enc_unit, enc_inverse, gain[0])
    dec_states = norm_back(dec_grad, dec_unit, dec_inverse, gain[1]) + grad_out.astype(jnp.float32)
    d_hidden = jnp.stack([enc_states, dec_states]).astype(jnp.bfloat16)
    result = jnp.stack([memory, output])
    return (result, d_hidden, d_gain, d_first, d_second)
```

```python
import functools
import math

import jax
import jax.numpy as jnp
from jax import lax
from jax.experimental import pallas as pl
from jax.experimental.pallas import tpu as pltpu
from jax.sharding import PartitionSpec as P

HEAD = 128
EPS = 1e-06
MASKED = -1e30
MESH = pl.DeviceIdType.MESH
BF = jnp.bfloat16
F32 = jnp.float32
NY = 4
NZ = 4
VMEM_LIMIT = 66_000_000


def spec(space):
    return pl.BlockSpec(memory_space=space)


def coords():
    d = lax.axis_index("dp")
    return d // (2 * NY), (d // 2) % NY, d % 2


def dp_of(xh, y, c):
    return (xh * NY + y) * 2 + c


def greet(peers):
    barrier = pltpu.get_barrier_semaphore()
    for peer in peers:
        pl.semaphore_signal(barrier, inc=1, device_id=peer, device_id_type=MESH)
    pl.semaphore_wait(barrier, len(peers))


def remote(src, dst, ssem, rsem, peer):
    return pltpu.make_async_remote_copy(
        src_ref=src, dst_ref=dst, send_sem=ssem, recv_sem=rsem, device_id=peer, device_id_type=MESH
    )


def gather_kernel(
    len_ref, hid_in, cot_in, gain_ref, wf_in, ws_in,
    wfull_out, act_out, proj_ref,
    w, hid, act, acc, ssem, rsem, lsem, osem,
):
    sec = lax.axis_index("section")
    xh, y, c = coords()
    oh = 1 - xh
    yp, ym, yf = (y + 1) % NY, (y + 3) % NY, (y + 2) % NY
    half = w.shape[3] // 2
    length, width = hid.shape
    pair = 2 * w.shape[3]
    sources = (wf_in, ws_in)

    partner = {"dp": dp_of(xh, y, 1 - c)}
    xpeer = {"dp": dp_of(oh, y, c)}
    up = {"dp": dp_of(xh, yp, c)}
    down = {"dp": dp_of(xh, ym, c)}

    low, high = pl.ds(0, half), pl.ds(half, half)
    kinds = (
        ((xh, y), None, xpeer),
        ((xh, y), None, up),
        ((xh, y), None, down),
        ((oh, y), None, up),
        ((oh, y), None, down),
        ((xh, ym), low, up),
        ((xh, yp), high, down),
        ((oh, ym), low, up),
        ((oh, yp), high, down),
        ((xh, y), None, partner),
        ((oh, y), None, partner),
        ((xh, ym), None, partner),
        ((xh, yp), None, partner),
        ((oh, ym), None, partner),
        ((oh, yp), None, partner),
        ((xh, yf), None, partner),
        ((oh, yf), None, partner),
    )
    own = (0, 1, 2, 9)

    def message(t, k):
        (h, yy), rows, peer = kinds[k]
        place = w.at[t, h * NY + yy, c]
        if rows is not None:
            place = w.at[t, h * NY + yy, c, rows]
        src = sources[t] if k in own else place
        return remote(src, place, ssem.at[t, k], rsem.at[t, k], peer)

    def start(t, *ks):
        for k in ks:
            message(t, k).start()

    def arrived(t, *ks):
        for k in ks:
            message(t, k).wait_recv()

    hid_copy = pltpu.make_async_copy(hid_in, hid, lsem.at[0])
    cot_copy = pltpu.make_async_copy(cot_in, act.at[1], lsem.at[1])
    own_copy = [
        pltpu.make_async_copy(sources[t], w.at[t, xh * NY + y, c], lsem.at[2 + t]) for t in range(2)
    ]
    hid_copy.start()
    cot_copy.start()
    for copy in own_copy:
        copy.start()
    greet([partner, xpeer, up, down])
    start(0, 0, 1, 2, 9)
    start(1, 0, 9)

    hid_copy.wait()
    cot_copy.wait()
    target_count = len_ref[0, 1]
    block = 16

    def norm_rows(i, carry):
        rows = pl.ds(pl.multiple_of(i * block, block), block)
        wide = hid[rows, :].astype(F32)
        inverse = lax.rsqrt(jnp.mean(wide * wide, axis=-1, keepdims=True) + EPS)
        act[0, rows, :] = (wide * inverse * gain_ref[...]).astype(BF)
        row = i * block + lax.broadcasted_iota(jnp.int32, (block, 1), 0)
        keep = jnp.logical_or(row < target_count, sec == 0)
        act[1, rows, :] = jnp.where(keep, act[1, rows, :].astype(F32), 0.0).astype(BF)
        return carry

    lax.fori_loop(0, length // block, norm_rows, 0)
    for copy in own_copy:
        copy.wait()

    saved = []

    def use(t, h, yy, first=False):
        p = h * NY + yy
        columns = pl.ds(pl.multiple_of(p * pair, 128), pair)
        copy = pltpu.make_async_copy(w.at[t, p], wfull_out.at[t, p], osem.at[len(saved)])
        copy.start()
        saved.append(copy)
        left = act[0, :, columns] if t == 0 else act[sec, :, columns]
        part = jnp.dot(left, w[t, p].reshape(pair, w.shape[4]), preferred_element_type=F32)
        if first:
            acc[t] = part
        else:
            acc[t] += part

    act_copy = pltpu.make_async_copy(act, act_out, lsem.at[4])
    act_copy.start()

    arrived(0, 1)
    start(0, 5, 11)
    arrived(0, 2)
    start(0, 6, 12)
    start(1, 1, 2)
    arrived(0, 9)
    use(0, xh, y, True)
    arrived(1, 9)
    use(1, xh, y, True)
    arrived(0, 0)
    start(0, 3, 4, 10)
    arrived(0, 11)
    use(0, xh, ym)
    arrived(0, 12)
    use(0, xh, yp)
    arrived(0, 5, 6)
    start(0, 15)
    arrived(0, 10)
    use(0, oh, y)
    arrived(1, 1)
    start(1, 5, 11)
    arrived(1, 2)
    start(1, 6, 12)
    arrived(0, 15)
    use(0, xh, yf)
    arrived(1, 0)
    start(1, 3, 4, 10)
    arrived(0, 3)
    start(0, 7, 13)
    arrived(0, 4)
    start(0, 8, 14)
    arrived(1, 11)
    use(1, xh, ym)
    arrived(1, 12)
    use(1, xh, yp)
    arrived(0, 13)
    use(0, oh, ym)
    arrived(0, 14)
    use(0, oh, yp)
    arrived(0, 7, 8)
    start(0, 16)
    arrived(1, 10)
    use(1, oh, y)
    arrived(1, 5, 6)
    start(1, 15)
    arrived(0, 16)
    use(0, oh, yf)
    proj_ref[0] = acc[0].astype(BF)
    arrived(1, 15)
    use(1, xh, yf)
    arrived(1, 3)
    start(1, 7, 13)
    arrived(1, 4)
    start(1, 8, 14)
    arrived(1, 13)
    use(1, oh, ym)
    arrived(1, 14)
    use(1, oh, yp)
    arrived(1, 7, 8)
    start(1, 16)
    arrived(1, 16)
    use(1, oh, yf)
    proj_ref[1] = acc[1].astype(BF)

    for t in range(2):
        for k in range(len(kinds)):
            message(t, k).wait_send()
    act_copy.wait()
    for copy in saved:
        copy.wait()


def gather_call(lengths, hidden, cotangent, gain, w_first, w_second):
    length, width = hidden.shape
    depth, columns = w_first.shape
    return pl.pallas_call(
        gather_kernel,
        out_shape=(
            jax.ShapeDtypeStruct((2, 2 * NY, 2, depth, columns), BF),
            jax.ShapeDtypeStruct((2, length, width), BF),
            jax.ShapeDtypeStruct((2, length, columns), BF),
        ),
        in_specs=[
            spec(pltpu.SMEM), spec(pl.ANY), spec(pl.ANY), spec(pltpu.VMEM), spec(pl.ANY), spec(pl.ANY),
        ],
        out_specs=(spec(pl.ANY), spec(pl.ANY), spec(pltpu.VMEM)),
        scratch_shapes=[
            pltpu.VMEM((2, 2 * NY, 2, depth, columns), BF),
            pltpu.VMEM((length, width), BF),
            pltpu.VMEM((2, length, width), BF),
            pltpu.VMEM((2, length, columns), F32),
            pltpu.SemaphoreType.DMA((2, 17)),
            pltpu.SemaphoreType.DMA((2, 17)),
            pltpu.SemaphoreType.DMA((5,)),
            pltpu.SemaphoreType.DMA((16,)),
        ],
        compiler_params=pltpu.CompilerParams(
            collective_id=0, has_side_effects=True, vmem_limit_bytes=VMEM_LIMIT
        ),
        name="gather_project",
    )(lengths, hidden, cotangent, gain, w_first, w_second)


def attend_kernel(len_ref, proj, out_ref, got, give, ssem, rsem):
    sec = lax.axis_index("section")
    other = {"section": 1 - sec}
    heads = proj.shape[2] // HEAD
    length = proj.shape[1]
    scale = 1.0 / math.sqrt(HEAD)
    greet([other])

    def columns(h):
        return pl.ds(h * HEAD, HEAD)

    def forward(h, i):
        return remote(
            proj.at[i, :, columns(h)], got.at[i, :, columns(h)], ssem.at[i, h], rsem.at[i, h], other
        )

    def backward(h, i):
        return remote(
            give.at[i, :, columns(h)], got.at[i, :, columns(h)], ssem.at[i, h], rsem.at[i, h], other
        )

    def nt(a, b):
        return lax.dot_general(a, b, (((1,), (1,)), ((), ())), preferred_element_type=F32)

    def tn(a, b):
        return lax.dot_general(a, b, (((0,), (0,)), ((), ())), preferred_element_type=F32)

    @pl.when(sec == 0)
    def _():
        for h in range(heads):
            forward(h, 0).start()
            forward(h, 1).start()
        for h in range(heads):
            for i in range(2):
                backward(h, i).wait_recv()
                out_ref[i, :, columns(h)] = got[i, :, columns(h)]
        for h in range(heads):
            for i in range(2):
                forward(h, i).wait_send()

    @pl.when(sec == 1)
    def _():
        visible = lax.broadcasted_iota(jnp.int32, (1, length), 1) < len_ref[0, 0]
        for h in range(heads):
            forward(h, 0).wait_recv()
            forward(h, 1).wait_recv()
            q = proj[0, :, columns(h)]
            gc = proj[1, :, columns(h)]
            k = got[0, :, columns(h)]
            v = got[1, :, columns(h)]
            scores = jnp.where(visible, nt(q, k) * scale, MASKED)
            top = jnp.max(scores, axis=-1, keepdims=True)
            e = jnp.exp(scores - top)
            weights = e / jnp.sum(e, axis=-1, keepdims=True)
            low = weights.astype(BF)
            grad_weights = nt(gc, v)
            inner = jnp.sum(weights * grad_weights, axis=-1, keepdims=True)
            grad_scores = (weights * (grad_weights - inner) * scale).astype(BF)
            give[0, :, columns(h)] = tn(grad_scores, q).astype(BF)
            give[1, :, columns(h)] = tn(low, gc).astype(BF)
            backward(h, 0).start()
            backward(h, 1).start()
            out_ref[0, :, columns(h)] = jnp.dot(grad_scores, k, preferred_element_type=F32).astype(BF)
            out_ref[1, :, columns(h)] = jnp.dot(low, v, preferred_element_type=F32).astype(BF)
        for h in range(heads):
            for i in range(2):
                backward(h, i).wait_send()


def attend_call(lengths, proj):
    heads = proj.shape[2] // HEAD
    return pl.pallas_call(
        attend_kernel,
        out_shape=jax.ShapeDtypeStruct(proj.shape, BF),
        in_specs=[spec(pltpu.SMEM), spec(pltpu.VMEM)],
        out_specs=spec(pltpu.VMEM),
        scratch_shapes=[
            pltpu.VMEM(proj.shape, BF),
            pltpu.VMEM(proj.shape, BF),
            pltpu.SemaphoreType.DMA((2, heads)),
            pltpu.SemaphoreType.DMA((2, heads)),
        ],
        compiler_params=pltpu.CompilerParams(collective_id=1, has_side_effects=True),
        name="attend_both",
    )(lengths, proj)


def reduce_kernel(
    hid_in, gain_ref, act_in, w_in, g,
    dw_ref, rows_out, gain_out,
    act, w, dwb, rp, rf, rn, xs, xr, zp, zf, zn, zo, hid, gz, gs,
    psem, prsem, fsem, frsem, nsem, nrsem, xsem, xrsem, zsem, zrsem, gsem, grsem, lsem,
):
    sec = lax.axis_index("section")
    z = lax.axis_index("mp")
    xh, y, c = coords()
    oh = 1 - xh
    yp, ym, yf = (y + 1) % NY, (y + 3) % NY, (y + 2) % NY
    zup, zdn, zfar = (z + 1) % NZ, (z + 3) % NZ, (z + 2) % NZ
    depth, columns = rp.shape[2:]
    half = depth // 2
    pair = 2 * depth
    length, width = act.shape[1:]
    rows = length // NZ
    hrows = rows // 2

    partner = {"dp": dp_of(xh, y, 1 - c)}
    xpeer = {"dp": dp_of(oh, y, c)}
    up = {"dp": dp_of(xh, yp, c)}
    down = {"dp": dp_of(xh, ym, c)}
    yfar = {"dp": dp_of(xh, yf, c)}
    above = {"mp": zup}
    below = {"mp": zdn}
    zopp = {"mp": zfar}

    act_copy = pltpu.make_async_copy(act_in, act, lsem.at[0])
    w_copy = pltpu.make_async_copy(w_in, w, lsem.at[1])
    hid_copy = pltpu.make_async_copy(
        hid_in.at[pl.ds(pl.multiple_of(z * rows, rows), rows)], hid, lsem.at[2]
    )
    act_copy.start()
    w_copy.start()
    hid_copy.start()
    greet([partner, xpeer, up, down, yfar, above, below, zopp])
    act_copy.wait()

    def to_partner(t, p):
        return remote(dwb.at[t, p, 1 - c], rp.at[t, p], psem.at[t, p], prsem.at[t, p], partner)

    def far_message(t, h, way):
        hh = oh if h == 0 else xh
        part = pl.ds(way * half, half)
        return remote(
            rp.at[t, hh * NY + yf, part], rf.at[t, h, way], fsem.at[t, h, way], frsem.at[t, h, way],
            up if way == 0 else down,
        )

    def near_message(t, h, way):
        hh = oh if h == 0 else xh
        return remote(
            rp.at[t, hh * NY + (yp if way == 0 else ym)], rn.at[t, h, way],
            nsem.at[t, h, way], nrsem.at[t, h, way], up if way == 0 else down,
        )

    def x_message(t):
        return remote(xs.at[t], xr.at[t], xsem.at[t], xrsem.at[t], xpeer)

    def products(hh, first, last):
        def body(j, carry):
            t = 1 - j % 2
            p = hh * NY + (y + 2 + j // 2) % NY
            left = act[t * sec, :, pl.ds(pl.multiple_of(p * pair, 128), pair)]
            out = lax.dot_general(left, g[t], (((0,), (0,)), ((), ())), preferred_element_type=F32)
            dwb[t, p] = out.astype(BF).reshape(2, depth, columns)
            to_partner(t, p).start()
            return carry

        lax.fori_loop(first, last, body, 0)

    def pair_sum(t, p, part=None):
        if part is None:
            part = pl.ds(0, depth)
        return dwb[t, p, c, part].astype(F32) + rp[t, p, part].astype(F32)

    def send_far(t, h):
        hh = oh if h == 0 else xh
        p = hh * NY + yf
        to_partner(t, p).wait_recv()
        rp[t, p] = pair_sum(t, p).astype(BF)
        far_message(t, h, 0).start()
        far_message(t, h, 1).start()

    def send_near(t, h):
        hh = oh if h == 0 else xh
        for way, yy in ((0, yp), (1, ym)):
            p = hh * NY + yy
            to_partner(t, p).wait_recv()
            far_message(t, h, way).wait_recv()
            mine, rest = pl.ds(way * half, half), pl.ds((1 - way) * half, half)
            rp[t, p, mine] = (pair_sum(t, p, mine) + rf[t, h, way].astype(F32)).astype(BF)
            rp[t, p, rest] = pair_sum(t, p, rest).astype(BF)
            near_message(t, h, way).start()

    def ring_total(t, h):
        hh = oh if h == 0 else xh
        p = hh * NY + y
        to_partner(t, p).wait_recv()
        near_message(t, h, 0).wait_recv()
        near_message(t, h, 1).wait_recv()
        return pair_sum(t, p) + rn[t, h, 0].astype(F32) + rn[t, h, 1].astype(F32)

    def z_rows(who, part=None):
        if part is None:
            return pl.ds(pl.multiple_of(who * rows, rows), rows)
        return pl.ds(pl.multiple_of(who * rows + part * hrows, hrows), hrows)

    def z_far(a, way):
        return remote(
            zp.at[a, z_rows(zfar, way)], zf.at[a, way], zsem.at[a, way], zrsem.at[a, way],
            above if way == 0 else below,
        )

    def z_near(a, way):
        return remote(
            zp.at[a, z_rows(zup if way == 0 else zdn)], zn.at[a, way], zsem.at[a, 2 + way],
            zrsem.at[a, 2 + way], above if way == 0 else below,
        )

    def z_own(a, way):
        place = zo.at[a, z_rows(z)]
        return remote(
            place, place, zsem.at[a, 4 + way], zrsem.at[a, 4 + way], above if way == 0 else below
        )

    def z_pass(a, way):
        place = zo.at[a, z_rows(zdn if way == 0 else zup, way)]
        return remote(
            place, place, zsem.at[a, 6 + way], zrsem.at[a, 6 + way], above if way == 0 else below
        )

    def head_product(a, terms):
        def body(p, carry):
            total = None
            for t in terms:
                right = w[t, p].reshape(pair, columns)
                part = lax.dot_general(g[t], right, (((1,), (1,)), ((), ())), preferred_element_type=F32)
                total = part if total is None else total + part
            zp[a, :, pl.ds(pl.multiple_of(p * pair, 128), pair)] = total.astype(BF)
            return carry

        lax.fori_loop(0, 2 * NY, body, 0)

    def z_send_near(a):
        for way, who in ((0, zup), (1, zdn)):
            z_far(a, way).wait_recv()
            place = z_rows(who, way)
            zp[a, place] = (zp[a, place].astype(F32) + zf[a, way].astype(F32)).astype(BF)
            z_near(a, way).start()

    def z_total(a, r, n):
        return (
            zp[a, pl.ds(pl.multiple_of(z * rows + r, n), n)].astype(F32)
            + zn[a, 0, pl.ds(r, n)].astype(F32)
            + zn[a, 1, pl.ds(r, n)].astype(F32)
        )

    def z_forward(a):
        for way in range(2):
            z_own(a, way).wait_recv()
            z_pass(a, way).start()

    block = 16

    def finish_output():
        z_near(0, 0).wait_recv()
        z_near(0, 1).wait_recv()

        def body(i, carry):
            r = pl.multiple_of(i * block, block)
            total = z_total(0, r, block) + hid[pl.ds(r, block)].astype(F32)
            zo[0, pl.ds(pl.multiple_of(z * rows + r, block), block)] = total.astype(BF)
            return carry

        lax.fori_loop(0, rows // block, body, 0)
        z_own(0, 0).start()
        z_own(0, 1).start()

    def finish_states():
        z_near(1, 0).wait_recv()
        z_near(1, 1).wait_recv()
        gains = gain_ref[...]

        def body(i, carry):
            r = pl.multiple_of(i * block, block)
            mine = pl.ds(pl.multiple_of(z * rows + r, block), block)
            wide = hid[pl.ds(r, block)].astype(F32)
            inverse = lax.rsqrt(jnp.mean(wide * wide, axis=-1, keepdims=True) + EPS)
            unit = wide * inverse
            extra = act[1, mine].astype(F32)
            grad = z_total(1, r, block) + jnp.where(sec == 0, extra, 0.0)
            scaled = grad * gains
            inner = jnp.mean(scaled * unit, axis=-1, keepdims=True)
            states = inverse * (scaled - unit * inner) + jnp.where(sec == 0, 0.0, extra)
            zo[1, mine] = states.astype(BF)
            gs[pl.ds(0, 1)] += jnp.sum(grad * unit, axis=0, keepdims=True)
            return carry

        gs[pl.ds(0, 1)] = jnp.zeros((1, width), F32)
        lax.fori_loop(0, rows // block, body, 0)
        for i in range(3):
            gain_z(i).start()
        z_own(1, 0).start()
        z_own(1, 1).start()

    gain_peers = (above, below, zopp, partner, xpeer, up, down, yfar)
    row0 = pl.ds(0, 1)

    def gain_z(i):
        return remote(gs.at[row0], gz.at[pl.ds(i, 1)], gsem.at[i], grsem.at[i], gain_peers[i])

    def gain_next(i, level):
        return remote(
            gs.at[pl.ds(level, 1)], gz.at[pl.ds(i, 1)], gsem.at[i], grsem.at[i], gain_peers[i]
        )

    products(oh, 0, 2)

    @pl.when(sec == 1)
    def _():
        w_copy.wait()
        head_product(0, (1,))
        z_far(0, 0).start()
        z_far(0, 1).start()

    send_far(1, 0)
    send_far(0, 0)
    products(oh, 2, 8)

    @pl.when(sec == 1)
    def _():
        head_product(1, (0,))
        z_send_near(0)

    @pl.when(sec == 0)
    def _():
        w_copy.wait()
        head_product(1, (0, 1))

    z_far(1, 0).start()
    z_far(1, 1).start()
    send_near(1, 0)
    send_near(0, 0)
    products(xh, 0, 2)
    send_far(1, 1)
    send_far(0, 1)
    products(xh, 2, 8)
    hid_copy.wait()

    @pl.when(sec == 1)
    def _():
        finish_output()

    z_send_near(1)
    for t in (1, 0):
        xs[t] = ring_total(t, 0).astype(BF)
        x_message(t).start()
    send_near(1, 1)
    send_near(0, 1)

    @pl.when(sec == 1)
    def _():
        z_forward(0)

    finish_states()
    z_forward(1)
    for i in range(3):
        gain_z(i).wait_recv()
    gs[pl.ds(1, 1)] = gs[row0] + gz[pl.ds(0, 1)] + gz[pl.ds(1, 1)] + gz[pl.ds(2, 1)]
    gain_next(3, 1).start()
    for t in (1, 0):
        total = ring_total(t, 1)
        x_message(t).wait_recv()
        dw_ref[t] = total + xr[t].astype(F32)
        if t == 1:
            gain_next(3, 1).wait_recv()
            gs[pl.ds(2, 1)] = gs[pl.ds(1, 1)] + gz[pl.ds(3, 1)]
            gain_next(4, 2).start()
    gain_next(4, 2).wait_recv()
    gs[pl.ds(3, 1)] = gs[pl.ds(2, 1)] + gz[pl.ds(4, 1)]
    for i in (5, 6, 7):
        gain_next(i, 3).start()
    for i in (5, 6, 7):
        gain_next(i, 3).wait_recv()
    gain_out[...] = gs[pl.ds(3, 1)] + gz[pl.ds(5, 1)] + gz[pl.ds(6, 1)] + gz[pl.ds(7, 1)]

    @pl.when(sec == 1)
    def _():
        z_pass(0, 0).wait_recv()
        z_pass(0, 1).wait_recv()
        out = pltpu.make_async_copy(zo.at[0], rows_out.at[0], lsem.at[3])
        out.start()
        out.wait()
        for way in range(2):
            for make in (z_far, z_near, z_own, z_pass):
                make(0, way).wait_send()

    @pl.when(sec == 0)
    def _():
        out = pltpu.make_async_copy(act.at[0], rows_out.at[0], lsem.at[3])
        out.start()
        out.wait()

    z_pass(1, 0).wait_recv()
    z_pass(1, 1).wait_recv()
    out = pltpu.make_async_copy(zo.at[1], rows_out.at[1], lsem.at[4])
    out.start()
    out.wait()
    for way in range(2):
        for make in (z_far, z_near, z_own, z_pass):
            make(1, way).wait_send()
    for i in range(3):
        gain_z(i).wait_send()
    for i, level in ((3, 1), (4, 2), (5, 3), (6, 3), (7, 3)):
        gain_next(i, level).wait_send()
    for t in range(2):
        x_message(t).wait_send()
        for h in range(2):
            for way in range(2):
                far_message(t, h, way).wait_send()
                near_message(t, h, way).wait_send()

    def drain(j, carry):
        to_partner(j % 2, j // 2).wait_send()
        return carry

    lax.fori_loop(0, 4 * NY, drain, 0)


def reduce_call(hidden, gain, act, w_full, g):
    length, width = hidden.shape
    depth, columns = w_full.shape[3:]
    rows = length // NZ
    dma = pltpu.SemaphoreType.DMA
    return pl.pallas_call(
        reduce_kernel,
        out_shape=(
            jax.ShapeDtypeStruct((2, depth, columns), F32),
            jax.ShapeDtypeStruct((2, length, width), BF),
            jax.ShapeDtypeStruct((1, width), F32),
        ),
        in_specs=[spec(pl.ANY), spec(pltpu.VMEM), spec(pl.ANY), spec(pl.ANY), spec(pltpu.VMEM)],
        out_specs=(spec(pltpu.VMEM), spec(pl.ANY), spec(pltpu.VMEM)),
        scratch_shapes=[
            pltpu.VMEM(act.shape, BF),
            pltpu.VMEM(w_full.shape, BF),
            pltpu.VMEM(w_full.shape, BF),
            pltpu.VMEM((2, 2 * NY, depth, columns), BF),
            pltpu.VMEM((2, 2, 2, depth // 2, columns), BF),
            pltpu.VMEM((2, 2, 2, depth, columns), BF),
            pltpu.VMEM((2, depth, columns), BF),
            pltpu.VMEM((2, depth, columns), BF),
            pltpu.VMEM((2, length, width), BF),
            pltpu.VMEM((2, 2, rows // 2, width), BF),
            pltpu.VMEM((2, 2, rows, width), BF),
            pltpu.VMEM((2, length, width), BF),
            pltpu.VMEM((rows, width), BF),
            pltpu.VMEM((8, width), F32),
            pltpu.VMEM((8, width), F32),
            dma((2, 2 * NY)), dma((2, 2 * NY)),
            dma((2, 2, 2)), dma((2, 2, 2)),
            dma((2, 2, 2)), dma((2, 2, 2)),
            dma((2,)), dma((2,)),
            dma((2, 8)), dma((2, 8)),
            dma((8,)), dma((8,)),
            dma((5,)),
        ],
        compiler_params=pltpu.CompilerParams(
            collective_id=2, has_side_effects=True, vmem_limit_bytes=VMEM_LIMIT
        ),
        name="reduce_all",
    )(hidden, gain, act, w_full, g)


def shards(hidden, gain, w_first, w_second, lengths, cotangent):
    states = hidden[0, 0]
    w_full, act, proj = gather_call(
        lengths, states, cotangent[0, 0], gain, w_first[0], w_second[0]
    )
    g = attend_call(lengths, proj)
    dw, rows, gain_sum = reduce_call(states, gain, act, w_full, g)
    depth = w_first.shape[1]
    gain_part = lax.dynamic_slice(gain_sum, (0, lax.axis_index("dp") * depth), (1, depth))
    return (rows[0][None, None], rows[1][None, None], gain_part, dw[0][None], dw[1][None])


def solution(mesh):
    return jax.shard_map(
        shards,
        mesh=mesh,
        in_specs=(
            P("section", "dp", None, None),
            P("section", None),
            P("section", "dp", "mp"),
            P("section", "dp", "mp"),
            P("dp", None),
            P("section", "dp", None, None),
        ),
        out_specs=(
            P("section", "dp", None, None),
            P("section", "dp", None, None),
            P("section", "dp"),
            P("section", "dp", "mp"),
            P("section", "dp", "mp"),
        ),
        check_vma=False,
    )
```

```python
import math

import jax
import jax.numpy as jnp
from jax import lax
from jax.experimental import pallas as pl
from jax.experimental.pallas import tpu as pltpu
from jax.sharding import PartitionSpec as P

HEAD = 128
EPS = 1e-06
MASKED = -1e30
MESH = pl.DeviceIdType.MESH
BF = jnp.bfloat16
F32 = jnp.float32
NY = 4
NZ = 4
VMEM_LIMIT = 67_000_000


def spec(space):
    return pl.BlockSpec(memory_space=space)


def coords():
    d = lax.axis_index("dp")
    return d // (2 * NY), (d // 2) % NY, d % 2


def dp_of(xh, y, c):
    return (xh * NY + y) * 2 + c


def greet(peers):
    barrier = pltpu.get_barrier_semaphore()
    for peer in peers:
        pl.semaphore_signal(barrier, inc=1, device_id=peer, device_id_type=MESH)
    pl.semaphore_wait(barrier, len(peers))


def remote(src, dst, ssem, rsem, peer):
    return pltpu.make_async_remote_copy(
        src_ref=src, dst_ref=dst, send_sem=ssem, recv_sem=rsem, device_id=peer, device_id_type=MESH
    )


def nt(a, b):
    return lax.dot_general(a, b, (((1,), (1,)), ((), ())), preferred_element_type=F32)


def tn(a, b):
    return lax.dot_general(a, b, (((0,), (0,)), ((), ())), preferred_element_type=F32)


def fused_kernel(
    len_ref, hid_in, cot_in, gain_ref, wf_in, ws_in,
    res_out, states_out, dw0_out, dw1_out, gain_out,
    w, act, acc, proj, grads, give, wgt,
    dwb, rp, rf, rn, xs, xr, zp, zf, zn, zs, hid, gz, gs,
    asem, arsem, bsem, brsem, psem, prsem, fsem, frsem, nsem, nrsem, xsem, xrsem,
    zsem, zrsem, gsem, grsem, lsem,
):
    sec = lax.axis_index("section")
    z = lax.axis_index("mp")
    xh, y, c = coords()
    oh = 1 - xh
    yp, ym, yf = (y + 1) % NY, (y + 3) % NY, (y + 2) % NY
    zup, zdn, zfar = (z + 1) % NZ, (z + 3) % NZ, (z + 2) % NZ
    depth, columns = rp.shape[2:]
    half = depth // 2
    pair = 2 * depth
    length, width = act.shape[1:]
    rows = length // NZ
    hrows = rows // 2
    heads = columns // HEAD
    scale = 1.0 / math.sqrt(HEAD)
    sources = (wf_in, ws_in)
    outs = (res_out, states_out)
    dw_outs = (dw0_out, dw1_out)
    block = 16

    partner = {"dp": dp_of(xh, y, 1 - c)}
    xpeer = {"dp": dp_of(oh, y, c)}
    up = {"dp": dp_of(xh, yp, c)}
    down = {"dp": dp_of(xh, ym, c)}
    yfar = {"dp": dp_of(xh, yf, c)}
    above = {"mp": zup}
    below = {"mp": zdn}
    zopp = {"mp": zfar}
    other = {"section": 1 - sec}

    low, high = pl.ds(0, half), pl.ds(half, half)
    kinds = (
        ((xh, y), None, xpeer),
        ((xh, y), None, up),
        ((xh, y), None, down),
        ((oh, y), None, up),
        ((oh, y), None, down),
        ((xh, ym), low, up),
        ((xh, yp), high, down),
        ((oh, ym), low, up),
        ((oh, yp), high, down),
        ((xh, y), None, partner),
        ((oh, y), None, partner),
        ((xh, ym), None, partner),
        ((xh, yp), None, partner),
        ((oh, ym), None, partner),
        ((oh, yp), None, partner),
        ((xh, yf), None, partner),
        ((oh, yf), None, partner),
    )
    own = (0, 1, 2, 9)

    def message(t, k):
        (h, yy), part, peer = kinds[k]
        place = w.at[t, h * NY + yy, c]
        if part is not None:
            place = w.at[t, h * NY + yy, c, part]
        src = sources[t] if k in own else place
        return remote(src, place, asem.at[t, k], arsem.at[t, k], peer)

    def start(t, *ks):
        for k in ks:
            message(t, k).start()

    def arrived(t, *ks):
        for k in ks:
            message(t, k).wait_recv()

    def use(t, h, yy, first=False):
        p = h * NY + yy
        cols = pl.ds(pl.multiple_of(p * pair, 128), pair)
        left = act[0, :, cols] if t == 0 else act[sec, :, cols]
        part = jnp.dot(left, w[t, p].reshape(pair, columns), preferred_element_type=F32)
        if first:
            acc[t, pl.ds(0, length)] = part
        else:
            acc[t, pl.ds(0, length)] += part

    def head(h):
        return pl.ds(h * HEAD, HEAD)

    def forward(h, i):
        return remote(
            proj.at[i, :, head(h)], grads.at[0, i, :, head(h)], bsem.at[i, h], brsem.at[i, h], other
        )

    def backward(h, i):
        return remote(
            give.at[i, :, head(h)], grads.at[0, i, :, head(h)], bsem.at[i, h], brsem.at[i, h], other
        )

    def to_partner(t, p):
        return remote(dwb.at[t, p, 1 - c], rp.at[t, p], psem.at[t, p], prsem.at[t, p], partner)

    def far_message(t, h, way):
        hh = oh if h == 0 else xh
        part = pl.ds(way * half, half)
        return remote(
            rp.at[t, hh * NY + yf, part], rf.at[t, h, way], fsem.at[t, h, way], frsem.at[t, h, way],
            up if way == 0 else down,
        )

    def near_message(t, h, way):
        hh = oh if h == 0 else xh
        return remote(
            rp.at[t, hh * NY + (yp if way == 0 else ym)], rn.at[t, h, way],
            nsem.at[t, h, way], nrsem.at[t, h, way], up if way == 0 else down,
        )

    def x_message(t):
        return remote(xs.at[t], xr.at[t], xsem.at[t], xrsem.at[t], xpeer)

    def products(t, h, first, last):
        hh = oh if h == 0 else xh

        def body(j, carry):
            p = hh * NY + (y + 2 + j) % NY
            left = act[t * sec, :, pl.ds(pl.multiple_of(p * pair, 128), pair)]
            dwb[t, p] = tn(left, grads[sec, t]).astype(BF).reshape(2, depth, columns)
            to_partner(t, p).start()
            return carry

        lax.fori_loop(first, last, body, 0)

    def pair_sum(t, p, part=None):
        if part is None:
            part = pl.ds(0, depth)
        return dwb[t, p, c, part].astype(F32) + rp[t, p, part].astype(F32)

    def send_far(t, h):
        hh = oh if h == 0 else xh
        p = hh * NY + yf
        to_partner(t, p).wait_recv()
        rp[t, p] = pair_sum(t, p).astype(BF)
        far_message(t, h, 0).start()
        far_message(t, h, 1).start()

    def send_near(t, h):
        hh = oh if h == 0 else xh
        for way, yy in ((0, yp), (1, ym)):
            p = hh * NY + yy
            to_partner(t, p).wait_recv()
            far_message(t, h, way).wait_recv()
            mine, rest = pl.ds(way * half, half), pl.ds((1 - way) * half, half)
            rp[t, p, mine] = (pair_sum(t, p, mine) + rf[t, h, way].astype(F32)).astype(BF)
            rp[t, p, rest] = pair_sum(t, p, rest).astype(BF)
            near_message(t, h, way).start()

    def ring_total(t, h):
        hh = oh if h == 0 else xh
        p = hh * NY + y
        to_partner(t, p).wait_recv()
        near_message(t, h, 0).wait_recv()
        near_message(t, h, 1).wait_recv()
        return pair_sum(t, p) + rn[t, h, 0].astype(F32) + rn[t, h, 1].astype(F32)

    def send_x(t):
        xs[t] = ring_total(t, 0).astype(BF)
        x_message(t).start()

    def dw_copy(t):
        return pltpu.make_async_copy(acc.at[t], dw_outs[t], lsem.at[6 + t])

    def finish_dw(t):
        total = ring_total(t, 1)
        x_message(t).wait_recv()
        acc[t] = total + xr[t].astype(F32)
        dw_copy(t).start()

    def z_rows(who, part=None):
        if part is None:
            return pl.ds(pl.multiple_of(who * rows, rows), rows)
        return pl.ds(pl.multiple_of(who * rows + part * hrows, hrows), hrows)

    def z_far(a, way):
        return remote(
            zp.at[a, z_rows(zfar, way)], zf.at[a, way], zsem.at[a, way], zrsem.at[a, way],
            above if way == 0 else below,
        )

    def z_near(a, way):
        return remote(
            zp.at[a, z_rows(zup if way == 0 else zdn)], zn.at[a, way], zsem.at[a, 2 + way],
            zrsem.at[a, 2 + way], above if way == 0 else below,
        )

    def z_own(a, way):
        return remote(
            zs.at[a], outs[a].at[z_rows(z)], zsem.at[a, 4 + way], zrsem.at[a, 4 + way],
            above if way == 0 else below,
        )

    def z_pass(a, way):
        place = outs[a].at[z_rows(zdn if way == 0 else zup, way)]
        return remote(
            place, place, zsem.at[a, 6 + way], zrsem.at[a, 6 + way], above if way == 0 else below
        )

    def z_keep(a):
        return pltpu.make_async_copy(zs.at[a], outs[a].at[z_rows(z)], lsem.at[4 + a])

    def head_product(a, terms):
        def body(p, carry):
            total = None
            for t in terms:
                part = nt(grads[sec, t], w[t, p].reshape(pair, columns))
                total = part if total is None else total + part
            zp[a, :, pl.ds(pl.multiple_of(p * pair, 128), pair)] = total.astype(BF)
            return carry

        lax.fori_loop(0, 2 * NY, body, 0)
        z_far(a, 0).start()
        z_far(a, 1).start()

    def z_send_near(a):
        for way, who in ((0, zup), (1, zdn)):
            z_far(a, way).wait_recv()
            place = z_rows(who, way)
            zp[a, place] = (zp[a, place].astype(F32) + zf[a, way].astype(F32)).astype(BF)
            z_near(a, way).start()

    def z_total(a, r):
        return (
            zp[a, pl.ds(pl.multiple_of(z * rows + r, block), block)].astype(F32)
            + zn[a, 0, pl.ds(r, block)].astype(F32)
            + zn[a, 1, pl.ds(r, block)].astype(F32)
        )

    def z_spread(a):
        z_own(a, 0).start()
        z_own(a, 1).start()
        z_keep(a).start()

    def z_forward(a):
        for way in range(2):
            z_own(a, way).wait_recv()
            z_pass(a, way).start()

    def finish_output():
        z_near(0, 0).wait_recv()
        z_near(0, 1).wait_recv()

        def body(i, carry):
            r = pl.multiple_of(i * block, block)
            zs[0, pl.ds(r, block)] = (z_total(0, r) + hid[pl.ds(r, block)].astype(F32)).astype(BF)
            return carry

        lax.fori_loop(0, rows // block, body, 0)
        z_spread(0)

    def finish_states():
        z_near(1, 0).wait_recv()
        z_near(1, 1).wait_recv()
        gains = gain_ref[...]

        def body(i, carry):
            r = pl.multiple_of(i * block, block)
            wide = hid[pl.ds(r, block)].astype(F32)
            inverse = lax.rsqrt(jnp.mean(wide * wide, axis=-1, keepdims=True) + EPS)
            unit = wide * inverse
            extra = act[1, pl.ds(pl.multiple_of(z * rows + r, block), block)].astype(F32)
            grad = z_total(1, r) + jnp.where(sec == 0, extra, 0.0)
            scaled = grad * gains
            inner = jnp.mean(scaled * unit, axis=-1, keepdims=True)
            states = inverse * (scaled - unit * inner) + jnp.where(sec == 0, 0.0, extra)
            zs[1, pl.ds(r, block)] = states.astype(BF)
            gs[pl.ds(0, 1)] += jnp.sum(grad * unit, axis=0, keepdims=True)
            return carry

        gs[pl.ds(0, 1)] = jnp.zeros((1, width), F32)
        lax.fori_loop(0, rows // block, body, 0)
        for i in range(3):
            gain_message(i, 0).start()
        z_spread(1)

    gain_peers = (above, below, zopp, partner, xpeer, up, down, yfar)

    def gain_message(i, level):
        return remote(
            gs.at[pl.ds(level, 1)], gz.at[pl.ds(i, 1)], gsem.at[i], grsem.at[i], gain_peers[i]
        )

    gain_steps = (((0, 1, 2), 0), ((3,), 1), ((4,), 2), ((5, 6, 7), 3))

    def gain_step(level):
        slots, _ = gain_steps[level]
        total = gs[pl.ds(level, 1)]
        for i in slots:
            gain_message(i, level).wait_recv()
            total = total + gz[pl.ds(i, 1)]
        if level == 3:
            gain_out[...] = total
            return
        gs[pl.ds(level + 1, 1)] = total
        for i in gain_steps[level + 1][0]:
            gain_message(i, level + 1).start()

    def encoder_tail():
        for h in range(heads):
            forward(h, 1).start()
        for h in range(heads):
            backward(h, 1).wait_recv()
        products(1, 0, 0, 2)
        send_far(1, 0)
        products(1, 0, 2, 4)
        products(1, 1, 0, 2)
        send_far(1, 1)
        products(1, 1, 2, 4)
        for h in range(heads):
            backward(h, 0).wait_recv()
        products(0, 0, 0, 2)
        send_far(0, 0)
        head_product(1, (0, 1))
        send_near(1, 0)
        products(0, 0, 2, 4)
        products(0, 1, 0, 2)
        send_far(0, 1)
        send_near(0, 0)
        products(0, 1, 2, 4)
        z_send_near(1)
        send_x(1)
        send_near(1, 1)
        send_x(0)
        send_near(0, 1)
        finish_states()
        z_forward(1)
        gain_step(0)
        gain_step(1)
        finish_dw(1)
        gain_step(2)
        finish_dw(0)
        gain_step(3)

    def softmax_part():
        visible = lax.broadcasted_iota(jnp.int32, (1, length), 1) < len_ref[0, 0]
        for h in range(heads):
            forward(h, 0).wait_recv()
            scores = nt(proj[0, :, head(h)], grads[0, 0, :, head(h)]) * scale
            scores = jnp.where(visible, scores, MASKED)
            e = jnp.exp(scores - jnp.max(scores, axis=-1, keepdims=True))
            wgt[h] = e / jnp.sum(e, axis=-1, keepdims=True)

    def decoder_tail():
        for h in range(heads):
            give[1, :, head(h)] = tn(wgt[h].astype(BF), proj[1, :, head(h)]).astype(BF)
            backward(h, 1).start()
        for h in range(heads):
            forward(h, 1).wait_recv()
            weights = wgt[h]
            v = grads[0, 1, :, head(h)]
            grad_weights = nt(proj[1, :, head(h)], v)
            inner = jnp.sum(weights * grad_weights, axis=-1, keepdims=True)
            grad_scores = (weights * (grad_weights - inner) * scale).astype(BF)
            give[0, :, head(h)] = tn(grad_scores, proj[0, :, head(h)]).astype(BF)
            backward(h, 0).start()
            grads[1, 1, :, head(h)] = jnp.dot(
                weights.astype(BF), v, preferred_element_type=F32
            ).astype(BF)
            grads[1, 0, :, head(h)] = jnp.dot(
                grad_scores, grads[0, 0, :, head(h)], preferred_element_type=F32
            ).astype(BF)
        head_product(0, (1,))
        products(1, 0, 0, 1)
        products(0, 0, 0, 1)
        send_far(1, 0)
        send_far(0, 0)
        head_product(1, (0,))
        products(1, 0, 1, 4)
        z_send_near(0)
        products(0, 0, 1, 4)
        send_near(1, 0)
        send_near(0, 0)
        products(1, 1, 0, 1)
        products(0, 1, 0, 1)
        send_far(1, 1)
        send_far(0, 1)
        z_send_near(1)
        products(1, 1, 1, 4)
        products(0, 1, 1, 4)
        finish_output()
        send_x(1)
        send_x(0)
        send_near(1, 1)
        send_near(0, 1)
        finish_states()
        z_forward(0)
        gain_step(0)
        gain_step(1)
        finish_dw(1)
        gain_step(2)
        finish_dw(0)
        gain_step(3)
        z_forward(1)

    hid_all = pltpu.make_async_copy(hid_in, zp.at[0], lsem.at[0])
    cot_copy = pltpu.make_async_copy(cot_in, act.at[1], lsem.at[1])
    own_copy = [
        pltpu.make_async_copy(sources[t], w.at[t, xh * NY + y, c], lsem.at[2 + t]) for t in range(2)
    ]
    hid_copy = pltpu.make_async_copy(
        hid_in.at[z_rows(z)], hid, lsem.at[8]
    )
    hid_all.start()
    cot_copy.start()
    for copy in own_copy:
        copy.start()
    hid_copy.start()
    greet([partner, xpeer, up, down, yfar, above, below, zopp, other])
    start(0, 0, 1, 2, 9)
    start(1, 0, 9)

    hid_all.wait()
    cot_copy.wait()
    target_count = len_ref[0, 1]

    def norm_rows(i, carry):
        r = pl.ds(pl.multiple_of(i * block, block), block)
        wide = zp[0, r, :].astype(F32)
        inverse = lax.rsqrt(jnp.mean(wide * wide, axis=-1, keepdims=True) + EPS)
        act[0, r, :] = (wide * inverse * gain_ref[...]).astype(BF)
        row = i * block + lax.broadcasted_iota(jnp.int32, (block, 1), 0)
        keep = jnp.logical_or(row < target_count, sec == 0)
        act[1, r, :] = jnp.where(keep, act[1, r, :].astype(F32), 0.0).astype(BF)
        return carry

    lax.fori_loop(0, length // block, norm_rows, 0)
    for copy in own_copy:
        copy.wait()
    hid_copy.wait()

    memory_copy = pltpu.make_async_copy(act.at[0], res_out, lsem.at[9])

    @pl.when(sec == 0)
    def _():
        memory_copy.start()

    arrived(0, 1)
    start(0, 5, 11)
    arrived(0, 2)
    start(0, 6, 12)
    start(1, 1, 2)
    arrived(0, 9)
    use(0, xh, y, True)
    arrived(1, 9)
    use(1, xh, y, True)
    arrived(0, 0)
    start(0, 3, 4, 10)
    arrived(0, 11)
    use(0, xh, ym)
    arrived(0, 12)
    use(0, xh, yp)
    arrived(0, 5, 6)
    start(0, 15)
    arrived(0, 10)
    use(0, oh, y)
    arrived(1, 1)
    start(1, 5, 11)
    arrived(1, 2)
    start(1, 6, 12)
    arrived(0, 15)
    use(0, xh, yf)
    arrived(1, 0)
    start(1, 3, 4, 10)
    arrived(0, 3)
    start(0, 7, 13)
    arrived(0, 4)
    start(0, 8, 14)
    arrived(1, 11)
    use(1, xh, ym)
    arrived(1, 12)
    use(1, xh, yp)
    arrived(0, 13)
    use(0, oh, ym)
    arrived(0, 14)
    use(0, oh, yp)
    arrived(0, 7, 8)
    start(0, 16)
    arrived(1, 10)
    use(1, oh, y)
    arrived(1, 5, 6)
    start(1, 15)
    arrived(0, 16)
    use(0, oh, yf)
    proj[0] = acc[0, pl.ds(0, length)].astype(BF)

    @pl.when(sec == 0)
    def _():
        for h in range(heads):
            forward(h, 0).start()

    arrived(1, 15)
    use(1, xh, yf)
    arrived(1, 3)
    start(1, 7, 13)
    arrived(1, 4)
    start(1, 8, 14)
    arrived(1, 13)
    use(1, oh, ym)
    arrived(1, 14)
    use(1, oh, yp)

    @pl.when(sec == 1)
    def _():
        softmax_part()

    arrived(1, 7, 8)
    start(1, 16)
    arrived(1, 16)
    use(1, oh, yf)
    proj[1] = acc[1, pl.ds(0, length)].astype(BF)

    @pl.when(sec == 0)
    def _():
        encoder_tail()

    @pl.when(sec == 1)
    def _():
        decoder_tail()

    @pl.when(sec == 0)
    def _():
        memory_copy.wait()
        for h in range(heads):
            for i in range(2):
                forward(h, i).wait_send()

    @pl.when(sec == 1)
    def _():
        for h in range(heads):
            for i in range(2):
                backward(h, i).wait_send()
        z_keep(0).wait()
        for way in range(2):
            z_pass(0, way).wait_recv()
            for make in (z_far, z_near, z_own, z_pass):
                make(0, way).wait_send()

    for t in range(2):
        for k in range(len(kinds)):
            message(t, k).wait_send()
    z_keep(1).wait()
    for way in range(2):
        z_pass(1, way).wait_recv()
        for make in (z_far, z_near, z_own, z_pass):
            make(1, way).wait_send()
    for slots, level in gain_steps:
        for i in slots:
            gain_message(i, level).wait_send()
    for t in range(2):
        dw_copy(t).wait()
        x_message(t).wait_send()
        for h in range(2):
            for way in range(2):
                far_message(t, h, way).wait_send()
                near_message(t, h, way).wait_send()

    def drain(j, carry):
        to_partner(j % 2, j // 2).wait_send()
        return carry

    lax.fori_loop(0, 4 * NY, drain, 0)


def fused_call(lengths, hidden, cotangent, gain, w_first, w_second):
    length, width = hidden.shape
    depth, columns = w_first.shape
    heads = columns // HEAD
    rows = length // NZ
    dma = pltpu.SemaphoreType.DMA
    return pl.pallas_call(
        fused_kernel,
        out_shape=(
            jax.ShapeDtypeStruct((length, width), BF),
            jax.ShapeDtypeStruct((length, width), BF),
            jax.ShapeDtypeStruct((depth, columns), F32),
            jax.ShapeDtypeStruct((depth, columns), F32),
            jax.ShapeDtypeStruct((1, width), F32),
        ),
        in_specs=[
            spec(pltpu.SMEM), spec(pl.ANY), spec(pl.ANY), spec(pltpu.VMEM), spec(pl.ANY), spec(pl.ANY),
        ],
        out_specs=(spec(pl.ANY), spec(pl.ANY), spec(pl.ANY), spec(pl.ANY), spec(pltpu.VMEM)),
        scratch_shapes=[
            pltpu.VMEM((2, 2 * NY, 2, depth, columns), BF),
            pltpu.VMEM((2, length, width), BF),
            pltpu.VMEM((2, depth, columns), F32),
            pltpu.VMEM((2, length, columns), BF),
            pltpu.VMEM((2, 2, length, columns), BF),
            pltpu.VMEM((2, length, columns), BF),
            pltpu.VMEM((heads, length, length), F32),
            pltpu.VMEM((2, 2 * NY, 2, depth, columns), BF),
            pltpu.VMEM((2, 2 * NY, depth, columns), BF),
            pltpu.VMEM((2, 2, 2, depth // 2, columns), BF),
            pltpu.VMEM((2, 2, 2, depth, columns), BF),
            pltpu.VMEM((2, depth, columns), BF),
            pltpu.VMEM((2, depth, columns), BF),
            pltpu.VMEM((2, length, width), BF),
            pltpu.VMEM((2, 2, rows // 2, width), BF),
            pltpu.VMEM((2, 2, rows, width), BF),
            pltpu.VMEM((2, rows, width), BF),
            pltpu.VMEM((rows, width), BF),
            pltpu.VMEM((8, width), F32),
            pltpu.VMEM((8, width), F32),
            dma((2, 17)), dma((2, 17)),
            dma((2, heads)), dma((2, heads)),
            dma((2, 2 * NY)), dma((2, 2 * NY)),
            dma((2, 2, 2)), dma((2, 2, 2)),
            dma((2, 2, 2)), dma((2, 2, 2)),
            dma((2,)), dma((2,)),
            dma((2, 8)), dma((2, 8)),
            dma((8,)), dma((8,)),
            dma((10,)),
        ],
        compiler_params=pltpu.CompilerParams(
            collective_id=0, has_side_effects=True, vmem_limit_bytes=VMEM_LIMIT
        ),
        name="fused_sublayer",
    )(lengths, hidden, cotangent, gain, w_first, w_second)


def shards(hidden, gain, w_first, w_second, lengths, cotangent):
    result, d_hidden, dw0, dw1, gain_sum = fused_call(
        lengths, hidden[0, 0], cotangent[0, 0], gain, w_first[0], w_second[0]
    )
    depth = w_first.shape[1]
    gain_part = lax.dynamic_slice(gain_sum, (0, lax.axis_index("dp") * depth), (1, depth))
    return (result[None, None], d_hidden[None, None], gain_part, dw0[None], dw1[None])


def solution(mesh):
    return jax.shard_map(
        shards,
        mesh=mesh,
        in_specs=(
            P("section", "dp", None, None),
            P("section", None),
            P("section", "dp", "mp"),
            P("section", "dp", "mp"),
            P("dp", None),
            P("section", "dp", None, None),
        ),
        out_specs=(
            P("section", "dp", None, None),
            P("section", "dp", None, None),
            P("section", "dp"),
            P("section", "dp", "mp"),
            P("section", "dp", "mp"),
        ),
        check_vma=False,
    )
```

```python
import math

import jax
import jax.numpy as jnp
from jax import lax
from jax.experimental import pallas as pl
from jax.experimental.pallas import tpu as pltpu
from jax.sharding import PartitionSpec as P

HEAD = 128
EPS = 1e-06
MASKED = -1e30
MESH = pl.DeviceIdType.MESH
BF = jnp.bfloat16
F32 = jnp.float32
NY = 4
NZ = 4
VMEM_LIMIT = 67_000_000


def spec(space):
    return pl.BlockSpec(memory_space=space)


def coords():
    d = lax.axis_index("dp")
    return d // (2 * NY), (d // 2) % NY, d % 2


def dp_of(xh, y, c):
    return (xh * NY + y) * 2 + c


def greet(peers):
    barrier = pltpu.get_barrier_semaphore()
    for peer in peers:
        pl.semaphore_signal(barrier, inc=1, device_id=peer, device_id_type=MESH)
    pl.semaphore_wait(barrier, len(peers))


def remote(src, dst, ssem, rsem, peer):
    return pltpu.make_async_remote_copy(
        src_ref=src, dst_ref=dst, send_sem=ssem, recv_sem=rsem, device_id=peer, device_id_type=MESH
    )


def nt(a, b):
    return lax.dot_general(a, b, (((1,), (1,)), ((), ())), preferred_element_type=F32)


def tn(a, b):
    return lax.dot_general(a, b, (((0,), (0,)), ((), ())), preferred_element_type=F32)


def fused_kernel(
    len_ref, hid_in, cot_in, gain_ref, wf_in, ws_in,
    res_out, states_out, dw0_out, dw1_out, gain_out,
    w, act, acc, proj, grads, give, wgt,
    dwb, rp, rf, rn, xs, xr, zp, zf, zn, zs, hid, gz, gs,
    asem, arsem, bsem, brsem, psem, prsem, fsem, frsem, nsem, nrsem, xsem, xrsem,
    zsem, zrsem, gsem, grsem, osem, orsem, lsem,
):
    sec = lax.axis_index("section")
    z = lax.axis_index("mp")
    xh, y, c = coords()
    oh = 1 - xh
    yp, ym, yf = (y + 1) % NY, (y + 3) % NY, (y + 2) % NY
    zup, zdn, zfar = (z + 1) % NZ, (z + 3) % NZ, (z + 2) % NZ
    depth, columns = rp.shape[2:]
    half = depth // 2
    pair = 2 * depth
    length, width = act.shape[1:]
    rows = length // NZ
    hrows = rows // 2
    heads = columns // HEAD
    scale = 1.0 / math.sqrt(HEAD)
    sources = (wf_in, ws_in)
    outs = (res_out, states_out)
    dw_outs = (dw0_out, dw1_out)
    block = 16

    partner = {"dp": dp_of(xh, y, 1 - c)}
    xpeer = {"dp": dp_of(oh, y, c)}
    up = {"dp": dp_of(xh, yp, c)}
    down = {"dp": dp_of(xh, ym, c)}
    yfar = {"dp": dp_of(xh, yf, c)}
    above = {"mp": zup}
    below = {"mp": zdn}
    zopp = {"mp": zfar}
    other = {"section": 1 - sec}

    low, high = pl.ds(0, half), pl.ds(half, half)
    kinds = (
        ((xh, y), None, xpeer),
        ((xh, y), None, up),
        ((xh, y), None, down),
        ((oh, y), None, up),
        ((oh, y), None, down),
        ((xh, ym), low, up),
        ((xh, yp), high, down),
        ((oh, ym), low, up),
        ((oh, yp), high, down),
        ((xh, y), None, partner),
        ((oh, y), None, partner),
        ((xh, ym), None, partner),
        ((xh, yp), None, partner),
        ((oh, ym), None, partner),
        ((oh, yp), None, partner),
        ((xh, yf), None, partner),
        ((oh, yf), None, partner),
    )
    own = (0, 1, 2, 9)

    def message(t, k):
        (h, yy), part, peer = kinds[k]
        place = w.at[t, h * NY + yy, c]
        if part is not None:
            place = w.at[t, h * NY + yy, c, part]
        src = sources[t] if k in own else place
        return remote(src, place, asem.at[t, k], arsem.at[t, k], peer)

    def start(t, *ks):
        for k in ks:
            message(t, k).start()

    def arrived(t, *ks):
        for k in ks:
            message(t, k).wait_recv()

    def use(t, h, yy, first=False):
        p = h * NY + yy
        cols = pl.ds(pl.multiple_of(p * pair, 128), pair)
        left = act[0, :, cols] if t == 0 else act[sec, :, cols]
        part = jnp.dot(left, w[t, p].reshape(pair, columns), preferred_element_type=F32)
        if first:
            acc[t, pl.ds(0, length)] = part
        else:
            acc[t, pl.ds(0, length)] += part

    def head(h):
        return pl.ds(h * HEAD, HEAD)

    def forward(h, i):
        return remote(
            proj.at[i, :, head(h)], grads.at[0, i, :, head(h)], bsem.at[i, h], brsem.at[i, h], other
        )

    def backward(h, i):
        return remote(
            give.at[i, :, head(h)], grads.at[0, i, :, head(h)], bsem.at[i, h], brsem.at[i, h], other
        )

    def to_partner(t, p):
        return remote(dwb.at[t, p, 1 - c], rp.at[t, p], psem.at[t, p], prsem.at[t, p], partner)

    def far_message(t, h, way):
        hh = oh if h == 0 else xh
        part = pl.ds(way * half, half)
        return remote(
            rp.at[t, hh * NY + yf, part], rf.at[t, h, way], fsem.at[t, h, way], frsem.at[t, h, way],
            up if way == 0 else down,
        )

    def near_message(t, h, way):
        hh = oh if h == 0 else xh
        return remote(
            rp.at[t, hh * NY + (yp if way == 0 else ym)], rn.at[t, h, way],
            nsem.at[t, h, way], nrsem.at[t, h, way], up if way == 0 else down,
        )

    def x_message(t):
        return remote(xs.at[t], xr.at[t], xsem.at[t], xrsem.at[t], xpeer)

    def products(t, h, first, last):
        hh = oh if h == 0 else xh

        def body(j, carry):
            p = hh * NY + (y + 2 + j) % NY
            left = act[t * sec, :, pl.ds(pl.multiple_of(p * pair, 128), pair)]
            dwb[t, p] = tn(left, grads[sec, t]).astype(BF).reshape(2, depth, columns)
            to_partner(t, p).start()
            return carry

        lax.fori_loop(first, last, body, 0)

    def pair_sum(t, p, part=None):
        if part is None:
            part = pl.ds(0, depth)
        return dwb[t, p, c, part].astype(F32) + rp[t, p, part].astype(F32)

    def send_far(t, h):
        hh = oh if h == 0 else xh
        p = hh * NY + yf
        to_partner(t, p).wait_recv()
        rp[t, p] = pair_sum(t, p).astype(BF)
        far_message(t, h, 0).start()
        far_message(t, h, 1).start()

    def send_near(t, h):
        hh = oh if h == 0 else xh
        for way, yy in ((0, yp), (1, ym)):
            p = hh * NY + yy
            to_partner(t, p).wait_recv()
            far_message(t, h, way).wait_recv()
            mine, rest = pl.ds(way * half, half), pl.ds((1 - way) * half, half)
            rp[t, p, mine] = (pair_sum(t, p, mine) + rf[t, h, way].astype(F32)).astype(BF)
            rp[t, p, rest] = pair_sum(t, p, rest).astype(BF)
            near_message(t, h, way).start()

    def ring_total(t, h):
        hh = oh if h == 0 else xh
        p = hh * NY + y
        to_partner(t, p).wait_recv()
        near_message(t, h, 0).wait_recv()
        near_message(t, h, 1).wait_recv()
        return pair_sum(t, p) + rn[t, h, 0].astype(F32) + rn[t, h, 1].astype(F32)

    def send_x(t):
        xs[t] = ring_total(t, 0).astype(BF)
        x_message(t).start()

    def dw_copy(t):
        return pltpu.make_async_copy(acc.at[t], dw_outs[t], lsem.at[6 + t])

    def finish_dw(t):
        total = ring_total(t, 1)
        x_message(t).wait_recv()
        acc[t] = total + xr[t].astype(F32)
        dw_copy(t).start()

    def z_rows(who, part=None):
        if part is None:
            return pl.ds(pl.multiple_of(who * rows, rows), rows)
        return pl.ds(pl.multiple_of(who * rows + part * hrows, hrows), hrows)

    def z_far(a, way):
        return remote(
            zp.at[a, z_rows(zfar, way)], zf.at[a, way], zsem.at[a, way], zrsem.at[a, way],
            above if way == 0 else below,
        )

    def z_near(a, way):
        return remote(
            zp.at[a, z_rows(zup if way == 0 else zdn)], zn.at[a, way], zsem.at[a, 2 + way],
            zrsem.at[a, 2 + way], above if way == 0 else below,
        )

    side = pl.ds(0, width // 2)

    def z_cols(a):
        return pl.ds(width // 2, width // 2) if a == 0 else pl.ds(0, width)

    def z_own(a, way):
        return remote(
            zs.at[a, :, z_cols(a)], outs[a].at[z_rows(z), z_cols(a)], zsem.at[a, 4 + way], zrsem.at[a, 4 + way],
            above if way == 0 else below,
        )

    def z_pass(a, way):
        place = outs[a].at[z_rows(zdn if way == 0 else zup, way), z_cols(a)]
        return remote(
            place, place, zsem.at[a, 6 + way], zrsem.at[a, 6 + way], above if way == 0 else below
        )

    def side_give():
        return remote(
            zs.at[0, :, side], zp.at[0, z_rows(z), side], osem.at[0], orsem.at[0], other
        )

    def side_own(way):
        place = zp.at[0, z_rows(z), side]
        return remote(
            place, place, osem.at[1 + way], orsem.at[1 + way], above if way == 0 else below
        )

    def side_pass(way):
        place = zp.at[0, z_rows(zdn if way == 0 else zup, way), side]
        return remote(
            place, place, osem.at[3 + way], orsem.at[3 + way], above if way == 0 else below
        )

    def side_back(way):
        r = z_rows(zdn if way == 0 else zup)
        return remote(
            zp.at[0, r, side], res_out.at[r, side], osem.at[5 + way], orsem.at[5 + way], other
        )

    def side_back_far(way):
        r = z_rows(zfar, way)
        return remote(
            zp.at[0, r, side], res_out.at[r, side], osem.at[7 + way], orsem.at[7 + way], other
        )

    def z_keep(a):
        return pltpu.make_async_copy(zs.at[a], outs[a].at[z_rows(z)], lsem.at[4 + a])

    def head_product(a, terms):
        def body(p, carry):
            total = None
            for t in terms:
                part = nt(grads[sec, t], w[t, p].reshape(pair, columns))
                total = part if total is None else total + part
            zp[a, :, pl.ds(pl.multiple_of(p * pair, 128), pair)] = total.astype(BF)
            return carry

        lax.fori_loop(0, 2 * NY, body, 0)
        z_far(a, 0).start()
        z_far(a, 1).start()

    def z_send_near(a):
        for way, who in ((0, zup), (1, zdn)):
            z_far(a, way).wait_recv()
            place = z_rows(who, way)
            zp[a, place] = (zp[a, place].astype(F32) + zf[a, way].astype(F32)).astype(BF)
            z_near(a, way).start()

    def z_total(a, r):
        return (
            zp[a, pl.ds(pl.multiple_of(z * rows + r, block), block)].astype(F32)
            + zn[a, 0, pl.ds(r, block)].astype(F32)
            + zn[a, 1, pl.ds(r, block)].astype(F32)
        )

    def z_spread(a):
        z_own(a, 0).start()
        z_own(a, 1).start()
        z_keep(a).start()

    def z_forward(a):
        for way in range(2):
            z_own(a, way).wait_recv()
            z_pass(a, way).start()

    def finish_output():
        z_near(0, 0).wait_recv()
        z_near(0, 1).wait_recv()

        def body(i, carry):
            r = pl.multiple_of(i * block, block)
            zs[0, pl.ds(r, block)] = (z_total(0, r) + hid[pl.ds(r, block)].astype(F32)).astype(BF)
            return carry

        lax.fori_loop(0, rows // block, body, 0)
        side_give().start()
        z_spread(0)

    def finish_states():
        z_near(1, 0).wait_recv()
        z_near(1, 1).wait_recv()
        gains = gain_ref[...]

        def body(i, carry):
            r = pl.multiple_of(i * block, block)
            wide = hid[pl.ds(r, block)].astype(F32)
            inverse = lax.rsqrt(jnp.mean(wide * wide, axis=-1, keepdims=True) + EPS)
            unit = wide * inverse
            extra = act[1, pl.ds(pl.multiple_of(z * rows + r, block), block)].astype(F32)
            grad = z_total(1, r) + jnp.where(sec == 0, extra, 0.0)
            scaled = grad * gains
            inner = jnp.mean(scaled * unit, axis=-1, keepdims=True)
            states = inverse * (scaled - unit * inner) + jnp.where(sec == 0, 0.0, extra)
            zs[1, pl.ds(r, block)] = states.astype(BF)
            gs[pl.ds(0, 1)] += jnp.sum(grad * unit, axis=0, keepdims=True)
            return carry

        gs[pl.ds(0, 1)] = jnp.zeros((1, width), F32)
        lax.fori_loop(0, rows // block, body, 0)
        for i in range(3):
            gain_message(i, 0).start()
        z_spread(1)

    gain_peers = (above, below, zopp, partner, xpeer, up, down, yfar)

    def gain_message(i, level):
        return remote(
            gs.at[pl.ds(level, 1)], gz.at[pl.ds(i, 1)], gsem.at[i], grsem.at[i], gain_peers[i]
        )

    gain_steps = (((0, 1, 2), 0), ((3,), 1), ((4,), 2), ((5, 6, 7), 3))

    def gain_step(level):
        slots, _ = gain_steps[level]
        total = gs[pl.ds(level, 1)]
        for i in slots:
            gain_message(i, level).wait_recv()
            total = total + gz[pl.ds(i, 1)]
        if level == 3:
            gain_out[...] = total
            return
        gs[pl.ds(level + 1, 1)] = total
        for i in gain_steps[level + 1][0]:
            gain_message(i, level + 1).start()

    def encoder_tail():
        for h in range(heads):
            forward(h, 1).start()
        for h in range(heads):
            backward(h, 1).wait_recv()
        products(1, 0, 0, 2)
        send_far(1, 0)
        products(1, 0, 2, 4)
        products(1, 1, 0, 2)
        send_far(1, 1)
        products(1, 1, 2, 4)
        for h in range(heads):
            backward(h, 0).wait_recv()
        products(0, 0, 0, 2)
        send_far(0, 0)
        head_product(1, (0, 1))
        send_near(1, 0)
        products(0, 0, 2, 4)
        products(0, 1, 0, 2)
        send_far(0, 1)
        send_near(0, 0)
        products(0, 1, 2, 4)
        z_send_near(1)
        send_x(1)
        send_near(1, 1)
        send_x(0)
        send_near(0, 1)
        finish_states()
        z_forward(1)
        side_give().wait_recv()
        side_own(0).start()
        side_own(1).start()
        gain_step(0)
        gain_step(1)
        for way in range(2):
            side_own(way).wait_recv()
            side_pass(way).start()
            side_back(way).start()
        finish_dw(1)
        for way in range(2):
            side_pass(way).wait_recv()
            side_back_far(way).start()
        gain_step(2)
        finish_dw(0)
        gain_step(3)

    def softmax_part():
        visible = lax.broadcasted_iota(jnp.int32, (1, length), 1) < len_ref[0, 0]
        for h in range(heads):
            forward(h, 0).wait_recv()
            scores = nt(proj[0, :, head(h)], grads[0, 0, :, head(h)]) * scale
            scores = jnp.where(visible, scores, MASKED)
            e = jnp.exp(scores - jnp.max(scores, axis=-1, keepdims=True))
            wgt[h] = e / jnp.sum(e, axis=-1, keepdims=True)

    def decoder_tail():
        for h in range(heads):
            give[1, :, head(h)] = tn(wgt[h].astype(BF), proj[1, :, head(h)]).astype(BF)
            backward(h, 1).start()
        for h in range(heads):
            forward(h, 1).wait_recv()
            weights = wgt[h]
            v = grads[0, 1, :, head(h)]
            grad_weights = nt(proj[1, :, head(h)], v)
            inner = jnp.sum(weights * grad_weights, axis=-1, keepdims=True)
            grad_scores = (weights * (grad_weights - inner) * scale).astype(BF)
            give[0, :, head(h)] = tn(grad_scores, proj[0, :, head(h)]).astype(BF)
            backward(h, 0).start()
            grads[1, 1, :, head(h)] = jnp.dot(
                weights.astype(BF), v, preferred_element_type=F32
            ).astype(BF)
            grads[1, 0, :, head(h)] = jnp.dot(
                grad_scores, grads[0, 0, :, head(h)], preferred_element_type=F32
            ).astype(BF)
        head_product(0, (1,))
        products(1, 0, 0, 1)
        products(0, 0, 0, 1)
        send_far(1, 0)
        send_far(0, 0)
        head_product(1, (0,))
        products(1, 0, 1, 4)
        z_send_near(0)
        products(0, 0, 1, 4)
        send_near(1, 0)
        send_near(0, 0)
        products(1, 1, 0, 1)
        products(0, 1, 0, 1)
        send_far(1, 1)
        send_far(0, 1)
        z_send_near(1)
        products(1, 1, 1, 4)
        products(0, 1, 1, 4)
        finish_output()
        send_x(1)
        send_x(0)
        send_near(1, 1)
        send_near(0, 1)
        finish_states()
        z_forward(0)
        gain_step(0)
        gain_step(1)
        finish_dw(1)
        gain_step(2)
        finish_dw(0)
        gain_step(3)
        z_forward(1)

    hid_all = pltpu.make_async_copy(hid_in, zp.at[0], lsem.at[0])
    cot_copy = pltpu.make_async_copy(cot_in, act.at[1], lsem.at[1])
    own_copy = [
        pltpu.make_async_copy(sources[t], w.at[t, xh * NY + y, c], lsem.at[2 + t]) for t in range(2)
    ]
    hid_copy = pltpu.make_async_copy(
        hid_in.at[z_rows(z)], hid, lsem.at[8]
    )
    hid_all.start()
    cot_copy.start()
    for copy in own_copy:
        copy.start()
    hid_copy.start()
    greet([partner, xpeer, up, down, yfar, above, below, zopp, other])
    start(0, 0, 1, 2, 9)
    start(1, 0, 9)

    hid_all.wait()
    cot_copy.wait()
    target_count = len_ref[0, 1]

    def norm_rows(i, carry):
        r = pl.ds(pl.multiple_of(i * block, block), block)
        wide = zp[0, r, :].astype(F32)
        inverse = lax.rsqrt(jnp.mean(wide * wide, axis=-1, keepdims=True) + EPS)
        act[0, r, :] = (wide * inverse * gain_ref[...]).astype(BF)
        row = i * block + lax.broadcasted_iota(jnp.int32, (block, 1), 0)
        keep = jnp.logical_or(row < target_count, sec == 0)
        act[1, r, :] = jnp.where(keep, act[1, r, :].astype(F32), 0.0).astype(BF)
        return carry

    lax.fori_loop(0, length // block, norm_rows, 0)
    for copy in own_copy:
        copy.wait()
    hid_copy.wait()

    memory_copy = pltpu.make_async_copy(act.at[0], res_out, lsem.at[9])

    @pl.when(sec == 0)
    def _():
        memory_copy.start()

    arrived(0, 1)
    start(0, 5, 11)
    arrived(0, 2)
    start(0, 6, 12)
    start(1, 1, 2)
    arrived(0, 9)
    use(0, xh, y, True)
    arrived(1, 9)
    use(1, xh, y, True)
    arrived(0, 0)
    start(0, 3, 4, 10)
    arrived(0, 11)
    use(0, xh, ym)
    arrived(0, 12)
    use(0, xh, yp)
    arrived(0, 5, 6)
    start(0, 15)
    arrived(0, 10)
    use(0, oh, y)
    arrived(1, 1)
    start(1, 5, 11)
    arrived(1, 2)
    start(1, 6, 12)
    arrived(0, 15)
    use(0, xh, yf)
    arrived(1, 0)
    start(1, 3, 4, 10)
    arrived(0, 3)
    start(0, 7, 13)
    arrived(0, 4)
    start(0, 8, 14)
    arrived(1, 11)
    use(1, xh, ym)
    arrived(1, 12)
    use(1, xh, yp)
    arrived(0, 13)
    use(0, oh, ym)
    arrived(0, 14)
    use(0, oh, yp)
    arrived(0, 7, 8)
    start(0, 16)
    arrived(1, 10)
    use(1, oh, y)
    arrived(1, 5, 6)
    start(1, 15)
    arrived(0, 16)
    use(0, oh, yf)
    proj[0] = acc[0, pl.ds(0, length)].astype(BF)

    @pl.when(sec == 0)
    def _():
        for h in range(heads):
            forward(h, 0).start()

    arrived(1, 15)
    use(1, xh, yf)
    arrived(1, 3)
    start(1, 7, 13)
    arrived(1, 4)
    start(1, 8, 14)
    arrived(1, 13)
    use(1, oh, ym)
    arrived(1, 14)
    use(1, oh, yp)

    @pl.when(sec == 1)
    def _():
        softmax_part()

    arrived(1, 7, 8)
    start(1, 16)
    arrived(1, 16)
    use(1, oh, yf)
    proj[1] = acc[1, pl.ds(0, length)].astype(BF)

    @pl.when(sec == 0)
    def _():
        encoder_tail()

    @pl.when(sec == 1)
    def _():
        decoder_tail()

    @pl.when(sec == 0)
    def _():
        memory_copy.wait()
        for way in range(2):
            for make in (side_own, side_pass, side_back, side_back_far):
                make(way).wait_send()
        for h in range(heads):
            for i in range(2):
                forward(h, i).wait_send()

    @pl.when(sec == 1)
    def _():
        for h in range(heads):
            for i in range(2):
                backward(h, i).wait_send()
        z_keep(0).wait()
        side_give().wait_send()
        for way in range(2):
            side_back(way).wait_recv()
            side_back_far(way).wait_recv()
        for way in range(2):
            z_pass(0, way).wait_recv()
            for make in (z_far, z_near, z_own, z_pass):
                make(0, way).wait_send()

    for t in range(2):
        for k in range(len(kinds)):
            message(t, k).wait_send()
    z_keep(1).wait()
    for way in range(2):
        z_pass(1, way).wait_recv()
        for make in (z_far, z_near, z_own, z_pass):
            make(1, way).wait_send()
    for slots, level in gain_steps:
        for i in slots:
            gain_message(i, level).wait_send()
    for t in range(2):
        dw_copy(t).wait()
        x_message(t).wait_send()
        for h in range(2):
            for way in range(2):
                far_message(t, h, way).wait_send()
                near_message(t, h, way).wait_send()

    def drain(j, carry):
        to_partner(j % 2, j // 2).wait_send()
        return carry

    lax.fori_loop(0, 4 * NY, drain, 0)


def fused_call(lengths, hidden, cotangent, gain, w_first, w_second):
    length, width = hidden.shape
    depth, columns = w_first.shape
    heads = columns // HEAD
    rows = length // NZ
    dma = pltpu.SemaphoreType.DMA
    return pl.pallas_call(
        fused_kernel,
        out_shape=(
            jax.ShapeDtypeStruct((length, width), BF),
            jax.ShapeDtypeStruct((length, width), BF),
            jax.ShapeDtypeStruct((depth, columns), F32),
            jax.ShapeDtypeStruct((depth, columns), F32),
            jax.ShapeDtypeStruct((1, width), F32),
        ),
        in_specs=[
            spec(pltpu.SMEM), spec(pl.ANY), spec(pl.ANY), spec(pltpu.VMEM), spec(pl.ANY), spec(pl.ANY),
        ],
        out_specs=(spec(pl.ANY), spec(pl.ANY), spec(pl.ANY), spec(pl.ANY), spec(pltpu.VMEM)),
        scratch_shapes=[
            pltpu.VMEM((2, 2 * NY, 2, depth, columns), BF),
            pltpu.VMEM((2, length, width), BF),
            pltpu.VMEM((2, depth, columns), F32),
            pltpu.VMEM((2, length, columns), BF),
            pltpu.VMEM((2, 2, length, columns), BF),
            pltpu.VMEM((2, length, columns), BF),
            pltpu.VMEM((heads, length, length), F32),
            pltpu.VMEM((2, 2 * NY, 2, depth, columns), BF),
            pltpu.VMEM((2, 2 * NY, depth, columns), BF),
            pltpu.VMEM((2, 2, 2, depth // 2, columns), BF),
            pltpu.VMEM((2, 2, 2, depth, columns), BF),
            pltpu.VMEM((2, depth, columns), BF),
            pltpu.VMEM((2, depth, columns), BF),
            pltpu.VMEM((2, length, width), BF),
            pltpu.VMEM((2, 2, rows // 2, width), BF),
            pltpu.VMEM((2, 2, rows, width), BF),
            pltpu.VMEM((2, rows, width), BF),
            pltpu.VMEM((rows, width), BF),
            pltpu.VMEM((8, width), F32),
            pltpu.VMEM((8, width), F32),
            dma((2, 17)), dma((2, 17)),
            dma((2, heads)), dma((2, heads)),
            dma((2, 2 * NY)), dma((2, 2 * NY)),
            dma((2, 2, 2)), dma((2, 2, 2)),
            dma((2, 2, 2)), dma((2, 2, 2)),
            dma((2,)), dma((2,)),
            dma((2, 8)), dma((2, 8)),
            dma((8,)), dma((8,)),
            dma((9,)), dma((9,)),
            dma((10,)),
        ],
        compiler_params=pltpu.CompilerParams(
            collective_id=0, has_side_effects=True, vmem_limit_bytes=VMEM_LIMIT
        ),
        name="fused_sublayer",
    )(lengths, hidden, cotangent, gain, w_first, w_second)


def shards(hidden, gain, w_first, w_second, lengths, cotangent):
    result, d_hidden, dw0, dw1, gain_sum = fused_call(
        lengths, hidden[0, 0], cotangent[0, 0], gain, w_first[0], w_second[0]
    )
    depth = w_first.shape[1]
    gain_part = lax.dynamic_slice(gain_sum, (0, lax.axis_index("dp") * depth), (1, depth))
    return (result[None, None], d_hidden[None, None], gain_part, dw0[None], dw1[None])


def solution(mesh):
    return jax.shard_map(
        shards,
        mesh=mesh,
        in_specs=(
            P("section", "dp", None, None),
            P("section", None),
            P("section", "dp", "mp"),
            P("section", "dp", "mp"),
            P("dp", None),
            P("section", "dp", None, None),
        ),
        out_specs=(
            P("section", "dp", None, None),
            P("section", "dp", None, None),
            P("section", "dp"),
            P("section", "dp", "mp"),
            P("section", "dp", "mp"),
        ),
        check_vma=False,
    )
```
